32 devices in a mesh: ia: 4 (over z), ja: 4 (over x, core), aux: 2 (over y).
Axes of the slice: x: 2, y: 2, z: 4, core: 2. Of those that a mesh axis runs over, the one named last changes fastest.
Arguments:
- raw_integrals: bfloat16 [2048, 12, 512], P(('ia', 'ja', 'aux')), may hold values from -0.5 to 0.5
- metric_root: bfloat16 [2048, 2048], replicated, may hold values from -0.125 to 0.125
- eps_occ: float32 [12], replicated, may hold values from -2 to -0.3
- eps_vir: float32 [512], replicated, may hold values from 0.3 to 3
Outputs:
- gamma: float32 [2048, 12, 512], P('ja', 'ia', 'aux')
The draws below stay inside these ranges and needn't reach their ends.
All inputs are finite; a program needn't handle non-finite values.
Results may differ from the reference program's by a relative error of at most 0.0022.
Values may be sent and summed in bfloat16 or wider, within the bound.
No kernel may reach another device: no remote copies, remote signals or barrier semaphores. Data moves between devices by JAX's collectives and lax.ppermute only.
A program may use at most 128 MiB of HBM per device.

```python
import math
import jax
import jax.numpy as jnp
from jax import lax

V = 512
NAUX = 2048
OCC = 12


def block_levels(own_key, shape, cuts, smallest, high):
    def one(dim, shards_of):
        heights = jax.random.uniform(jax.random.fold_in(jax.random.fold_in(own_key, 6), dim), (shards_of,), jnp.float32, smallest / len(cuts), high / len(cuts))
        return jnp.repeat(jnp.exp(heights), shape[dim] // shards_of).reshape((-1,) + (1,) * (len(shape) - dim - 1))

    gain = one(*cuts[0])
    for cut in cuts[1:]:
        gain = gain * one(*cut)
    return gain


def gaussian(rng, extent, scale, limit, cuts=(), held_as=jnp.bfloat16):
    result = jax.random.normal(rng, extent, jnp.float32) * scale
    if len(cuts) > 0:
        result = block_levels(rng, extent, cuts, -0.22, 0.18) * result
    return jnp.clip(result, min=-limit, max=limit).astype(held_as)


def setup_inputs(seed: int = 0) -> dict:
    key_of = jax.random.split(jax.random.key(seed), 5)
    raw_integrals = gaussian(key_of[0], (NAUX, OCC, V), 0.07, 0.5, ((0, 32),))
    metric_root = gaussian(key_of[1], (NAUX, NAUX), NAUX ** -0.5, 0.125)
    eps_occ = jnp.clip(jax.random.uniform(key_of[2], (OCC,), jnp.float32, -2.0, -0.3), -2.0, -0.3)
    eps_vir = jnp.clip(jnp.exp(jax.random.uniform(key_of[3], (V,), jnp.float32, math.log(0.3), math.log(3.0))), 0.3, 3.0)
    return {"raw_integrals": raw_integrals, "metric_root": metric_root, "eps_occ": eps_occ, "eps_vir": eps_vir}


def reference(raw_integrals, metric_root, eps_occ, eps_vir):
    fitted = lax.dot_general(metric_root, raw_integrals.reshape(NAUX, OCC * V), (((0,), (0,)), ((), ())), preferred_element_type=jnp.float32).astype(jnp.bfloat16)
    fitted_flat = fitted.astype(jnp.float32)

    def per_occupied(index):
        column = lax.dynamic_slice_in_dim(fitted_flat, (index * V).astype(jnp.int32), V, 1)
        coulomb = jnp.dot(column.T, fitted_flat, preferred_element_type=jnp.float32).reshape(V, OCC, V)
        energy_i = lax.dynamic_index_in_dim(eps_occ, index, 0, keepdims=False)
        denominator = eps_vir[:, None, None] + eps_vir[None, None, :] - energy_i - eps_occ[None, :, None]
        amplitude = ((2.0 * coulomb - coulomb.transpose(2, 1, 0)) / denominator).astype(jnp.bfloat16)
        amplitude = lax.optimization_barrier(amplitude).astype(jnp.float32)
        return jnp.dot(fitted_flat, amplitude.reshape(V, OCC * V).T, preferred_element_type=jnp.float32)

    gamma = lax.map(per_occupied, jnp.arange(OCC, dtype=jnp.int32))
    return gamma.transpose(1, 0, 2)
```

```python
import jax
import jax.numpy as jnp
from jax import lax
from jax.sharding import PartitionSpec as P

AXES = ("ia", "ja", "aux")
F32 = jnp.float32
BF16 = jnp.bfloat16


def low_bit(m):
    return m & -m


def high_bit(m):
    return 1 << (m.bit_length() - 1)


def dot(a, b, ca, cb):
    return lax.dot_general(a, b, (((ca,), (cb,)), ((), ())), preferred_element_type=F32)


class Grid:
    def __init__(self, mesh):
        self.nz = mesh.shape["ia"]
        self.nx = mesh.shape["ja"] // 2
        self.ny = mesh.shape["aux"]
        for n in (self.nz, self.nx, self.ny):
            assert n & (n - 1) == 0
        self.np = self.nx * self.ny

    def index(self, z, x, c, y):
        return ((z * self.nx + x) * 2 + c) * self.ny + y

    def swap(self, v, mz=0, mp=0, mc=0):
        mx, my = mp // self.ny, mp % self.ny
        pairs = [
            (self.index(z, x, c, y), self.index(z ^ mz, x ^ mx, c ^ mc, y ^ my))
            for z in range(self.nz)
            for x in range(self.nx)
            for c in range(2)
            for y in range(self.ny)
        ]
        return lax.ppermute(v, AXES, pairs)


def make_body(grid):
    nz, nx, ny, np_ = grid.nz, grid.nx, grid.ny, grid.np

    def body(raw_integrals, metric_root, eps_occ, eps_vir):
        pieces, occ, virt = raw_integrals.shape
        aux_total = metric_root.shape[0]
        ob_i, ob_j = occ // nz, occ // np_
        half = virt // 2
        z = lax.axis_index("ia")
        x, c = lax.axis_index("ja") // 2, lax.axis_index("ja") % 2
        y = lax.axis_index("aux")
        plane = x * ny + y

        mz, mp, mc = jnp.meshgrid(jnp.arange(nz), jnp.arange(np_), jnp.arange(2), indexing="ij")
        owner = (((z ^ mz) * nx + (x ^ (mp // ny))) * 2 + (c ^ mc)) * ny + (y ^ (mp % ny))
        metric = metric_root.reshape(-1, pieces, aux_total)[owner.reshape(-1)]
        metric = metric.reshape(aux_total, aux_total)

        raw = raw_integrals.transpose(1, 0, 2)
        own = lax.dynamic_slice_in_dim(raw, c * half, half, 2)
        other = lax.dynamic_slice_in_dim(raw, (1 - c) * half, half, 2)
        both = jnp.stack([own, grid.swap(other, mc=1)])

        def occ_block(index, size):
            return lax.dynamic_slice_in_dim(both, index * size, size, 1)

        rows = [occ_block(z, ob_i)]
        for m in range(1, nz):
            rows.append(grid.swap(occ_block(z ^ m, ob_i), mz=m))
        cols = [occ_block(plane, ob_j)]
        for m in range(1, np_):
            target = (x ^ (m // ny)) * ny + (y ^ (m % ny))
            cols.append(grid.swap(occ_block(target, ob_j), mp=m))

        def gather_z(block):
            got = [block]
            for m in range(1, nz):
                got.append(grid.swap(got[m ^ low_bit(m)], mz=low_bit(m)))
            return got

        raw_j = []
        for j in range(ob_j):
            block = jnp.stack([v[:, j] for v in cols])
            block = block.reshape(np_ * 2 * pieces, half)
            raw_j.append(gather_z(block))

        rows = jnp.stack(rows)
        cut = nz // 2
        got = {0: (rows[:cut], rows[cut:])}
        for m in range(1, np_):
            if m == low_bit(m):
                full = grid.swap(rows, mp=m)
                got[m] = (full[:cut], full[cut:])
            else:
                lo, hi = low_bit(m), high_bit(m)
                got[m] = (grid.swap(got[m ^ lo][0], mp=lo), grid.swap(got[m ^ hi][1], mp=hi))
        parts = [
            jnp.stack([got[m][h] for m in range(np_)], axis=1) for h in range(2)
        ]
        raw_i = jnp.concatenate(parts, axis=0)
        raw_i = raw_i.transpose(3, 0, 1, 2, 4, 5).reshape(ob_i, aux_total, half)

        def fit(block):
            return dot(block, metric, 0, 0).astype(BF16)

        fit_i = [fit(raw_i[i]) for i in range(ob_i)]
        fit_i_other = [grid.swap(f, mc=1) for f in fit_i]
        fit_j = [fit(jnp.concatenate(raw_j[j], axis=0)) for j in range(ob_j)]
        fit_j_other = [grid.swap(f, mc=1) for f in fit_j]

        eps_own = lax.dynamic_slice_in_dim(eps_vir, c * half, half, 0)
        eps_oth = lax.dynamic_slice_in_dim(eps_vir, (1 - c) * half, half, 0)
        eps_b = jnp.concatenate([eps_own, eps_oth])
        eps_i = lax.dynamic_slice_in_dim(eps_occ, z * ob_i, ob_i, 0)
        eps_j = lax.dynamic_slice_in_dim(eps_occ, plane * ob_j, ob_j, 0)

        q_rows = aux_total // (2 * nx)
        rows_own = jnp.concatenate(fit_i, axis=0)
        rows_oth = jnp.concatenate(fit_i_other, axis=0)
        own_total = oth_total = None
        for j in range(ob_j):
            col = jnp.concatenate([fit_j[j], fit_j_other[j]], axis=0)
            direct = dot(rows_own, col, 1, 1).reshape(ob_i, half, virt)
            swap_own = dot(rows_own, fit_j[j], 1, 1).reshape(ob_i, half, half)
            swap_oth = dot(rows_oth, fit_j[j], 1, 1).reshape(ob_i, half, half)
            swapped = jnp.concatenate([swap_own, swap_oth], axis=1).transpose(0, 2, 1)
            denominator = (
                eps_own[None, :, None] + eps_b[None, None, :] - eps_i[:, None, None] - eps_j[j]
            )
            amp = ((2.0 * direct - swapped) / denominator).astype(BF16)
            flipped = jnp.concatenate([amp[..., half:], amp[..., :half]], axis=2)
            amp_oth = grid.swap(flipped, mc=1)
            mine = lax.dynamic_index_in_dim(
                col.reshape(virt, nx, 2, q_rows), c, 2, keepdims=False
            ).reshape(virt, nx * q_rows)
            own_part = dot(mine, amp.reshape(ob_i * half, virt), 0, 1)
            oth_part = dot(mine, amp_oth.reshape(ob_i * half, virt), 0, 1)
            own_total = own_part if own_total is None else own_total + own_part
            oth_total = oth_part if oth_total is None else oth_total + oth_part

        total = jnp.stack([own_total, oth_total]).reshape(2, nx, q_rows, ob_i * half)
        if ny == 2:
            first = jnp.where(y == c, 0, 1)
        mid = q_rows // 2

        def pick(v, axis, index):
            return lax.dynamic_index_in_dim(v, index, axis, keepdims=False)

        a_rows = total[:, :, :mid]
        a_sum = pick(a_rows, 1, x)
        for m in range(1, nx):
            a_sum = a_sum + grid.swap(pick(a_rows, 1, x ^ m).astype(BF16), mp=m * ny).astype(F32)
        a_out = pick(a_sum, 0, first) + grid.swap(
            pick(a_sum, 0, 1 - first).astype(BF16), mp=1
        ).astype(F32)
        b_rows = total[:, :, mid:]
        b_sum = pick(b_rows, 0, first) + grid.swap(
            pick(b_rows, 0, 1 - first).astype(BF16), mp=1
        ).astype(F32)
        b_out = pick(b_sum, 0, x)
        for m in range(1, nx):
            b_out = b_out + grid.swap(pick(b_sum, 0, x ^ m).astype(BF16), mp=m * ny).astype(F32)
        out = jnp.concatenate([a_out, b_out], axis=0)
        return out.reshape(q_rows, ob_i, half)

    return body


def solution(mesh):
    body = make_body(Grid(mesh))
    in_specs = (P(AXES, None, None), P(), P(), P())
    return jax.shard_map(
        body, mesh=mesh, in_specs=in_specs, out_specs=P("ja", "ia", "aux"), check_vma=False
    )
```

```python
import jax
import jax.numpy as jnp
from jax import lax
from jax.experimental import pallas as pl
from jax.experimental.pallas import tpu as pltpu
from jax.sharding import PartitionSpec as P

AXES = ("ia", "ja", "aux")
F32 = jnp.float32
BF16 = jnp.bfloat16


def low_bit(m):
    return m & -m


def high_bit(m):
    return 1 << (m.bit_length() - 1)


def dot(a, b, ca, cb):
    return lax.dot_general(a, b, (((ca,), (cb,)), ((), ())), preferred_element_type=F32)


class Grid:
    def __init__(self, mesh):
        self.nz = mesh.shape["ia"]
        self.nx = mesh.shape["ja"] // 2
        self.ny = mesh.shape["aux"]
        for n in (self.nz, self.nx, self.ny):
            assert n & (n - 1) == 0
        self.np = self.nx * self.ny

    def index(self, z, x, c, y):
        return ((z * self.nx + x) * 2 + c) * self.ny + y

    def swap(self, v, mz=0, mp=0, mc=0):
        mx, my = mp // self.ny, mp % self.ny
        pairs = [
            (self.index(z, x, c, y), self.index(z ^ mz, x ^ mx, c ^ mc, y ^ my))
            for z in range(self.nz)
            for x in range(self.nx)
            for c in range(2)
            for y in range(self.ny)
        ]
        return lax.ppermute(v, AXES, pairs)


NT = (((1,), (1,)), ((), ()))


def amplitude(rows_own, rows_oth, col_own, col_oth, eps_own, eps_b, eps_i, eps_j):
    ob_i, half, aux_total = rows_own.shape

    def kernel(e_ref, ro, rx, co, cx, ea, eb, out):
        def mm(p, q):
            return lax.dot_general(p, q, NT, preferred_element_type=F32)

        ei = e_ref[pl.program_id(0)]
        ej = e_ref[ob_i]
        for k, (row, col) in enumerate(((ro, co), (rx, cx))):
            direct = mm(ro[0], col[...])
            swapped = mm(co[...], row[0])
            den = ea[...] + eb[:, k * half : (k + 1) * half] - ei - ej
            out[0, :, k * half : (k + 1) * half] = ((2.0 * direct - swapped) / den).astype(BF16)

    row_spec = pl.BlockSpec((1, half, aux_total), lambda i: (i, 0, 0))
    col_spec = pl.BlockSpec((half, aux_total), lambda i: (0, 0))
    return pl.pallas_call(
        kernel,
        grid=(ob_i,),
        out_shape=jax.ShapeDtypeStruct((ob_i, half, 2 * half), BF16),
        in_specs=[
            pl.BlockSpec(memory_space=pltpu.SMEM),
            row_spec,
            row_spec,
            col_spec,
            col_spec,
            pl.BlockSpec((half, 1), lambda i: (0, 0)),
            pl.BlockSpec((1, 2 * half), lambda i: (0, 0)),
        ],
        out_specs=pl.BlockSpec((1, half, 2 * half), lambda i: (i, 0, 0)),
        compiler_params=pltpu.CompilerParams(vmem_limit_bytes=24 << 20),
        cost_estimate=pl.CostEstimate(
            flops=8 * ob_i * half * half * aux_total,
            bytes_accessed=4 * ob_i * half * aux_total,
            transcendentals=0,
        ),
        name="amplitude",
    )(
        jnp.concatenate([eps_i, eps_j[None]]),
        rows_own,
        rows_oth,
        col_own,
        col_oth,
        eps_own[:, None],
        eps_b[None, :],
    )


def gamma_terms(where, fits, amps, i, nx, q_rows):
    half = fits[0][0].shape[0]
    nj = len(fits)
    cut = half // 2

    def kernel(w, *refs):
        cols, rows = refs[: 2 * nj], refs[2 * nj : 4 * nj]
        keep_x, send_x, keep_y, send_y = refs[4 * nj :]
        step = pl.program_id(0)
        for h in range(2):
            slot = w[2] ^ h
            acc = None
            for j in range(nj):
                amp = rows[2 * j + h]
                for k in range(2):
                    term = jnp.dot(
                        amp[0, :, k * half : (k + 1) * half],
                        cols[2 * j + (k ^ h)][...],
                        preferred_element_type=F32,
                    )
                    acc = term if acc is None else acc + term

            @pl.when(step == 0)
            def _():
                keep_x[slot] = acc[:cut]

            @pl.when(step > 0)
            def _():
                send_x[0, slot] = acc[:cut].astype(BF16)

            @pl.when(slot == 0)
            def _():
                keep_y[0] = acc[cut:]

            @pl.when(slot == 1)
            def _():
                send_y[0] = acc[cut:].astype(BF16)

    col_spec = pl.BlockSpec((half, q_rows), lambda s, w: (0, (w[0] ^ s) * 2 + w[1]))
    row_spec = pl.BlockSpec((1, half, 2 * half), lambda s, w: (i, 0, 0))
    flat_cols = [f for pair in fits for f in pair]
    flat_rows = [a for pair in amps for a in pair]
    return pl.pallas_call(
        kernel,
        grid_spec=pltpu.PrefetchScalarGridSpec(
            num_scalar_prefetch=1,
            grid=(nx,),
            in_specs=[col_spec] * (2 * nj) + [row_spec] * (2 * nj),
            out_specs=[
                pl.BlockSpec((2, cut, q_rows), lambda s, w: (0, 0, 0)),
                pl.BlockSpec((1, 2, cut, q_rows), lambda s, w: (jnp.maximum(s - 1, 0), 0, 0, 0)),
                pl.BlockSpec((1, cut, q_rows), lambda s, w: (s, 0, 0)),
                pl.BlockSpec((1, cut, q_rows), lambda s, w: (s, 0, 0)),
            ],
        ),
        out_shape=[
            jax.ShapeDtypeStruct((2, cut, q_rows), F32),
            jax.ShapeDtypeStruct((nx - 1, 2, cut, q_rows), BF16),
            jax.ShapeDtypeStruct((nx, cut, q_rows), F32),
            jax.ShapeDtypeStruct((nx, cut, q_rows), BF16),
        ],
        compiler_params=pltpu.CompilerParams(vmem_limit_bytes=24 << 20),
        cost_estimate=pl.CostEstimate(
            flops=8 * nx * nj * half * half * q_rows,
            bytes_accessed=12 * nj * half * half,
            transcendentals=0,
        ),
        name="gamma_terms",
    )(where, *flat_cols, *flat_rows)


def make_body(grid):
    nz, nx, ny, np_ = grid.nz, grid.nx, grid.ny, grid.np

    def body(raw_integrals, metric_root, eps_occ, eps_vir):
        pieces, occ, virt = raw_integrals.shape
        aux_total = metric_root.shape[0]
        ob_i, ob_j = occ // nz, occ // np_
        half = virt // 2
        z = lax.axis_index("ia")
        x, c = lax.axis_index("ja") // 2, lax.axis_index("ja") % 2
        y = lax.axis_index("aux")
        plane = x * ny + y

        mz, mp, mc = jnp.meshgrid(jnp.arange(nz), jnp.arange(np_), jnp.arange(2), indexing="ij")
        owner = (((z ^ mz) * nx + (x ^ (mp // ny))) * 2 + (c ^ mc)) * ny + (y ^ (mp % ny))
        metric = metric_root.reshape(-1, pieces, aux_total)[owner.reshape(-1)]
        metric = metric.reshape(aux_total, aux_total)

        raw = raw_integrals.transpose(1, 0, 2)
        own = lax.dynamic_slice_in_dim(raw, c * half, half, 2)
        other = lax.dynamic_slice_in_dim(raw, (1 - c) * half, half, 2)
        both = jnp.stack([own, grid.swap(other, mc=1)])

        def occ_block(index, size):
            return lax.dynamic_slice_in_dim(both, index * size, size, 1)

        rows = [occ_block(z, ob_i)]
        for m in range(1, nz):
            rows.append(grid.swap(occ_block(z ^ m, ob_i), mz=m))
        cols = [occ_block(plane, ob_j)]
        for m in range(1, np_):
            target = (x ^ (m // ny)) * ny + (y ^ (m % ny))
            cols.append(grid.swap(occ_block(target, ob_j), mp=m))

        def gather_z(block):
            got = [block]
            for m in range(1, nz):
                got.append(grid.swap(got[m ^ low_bit(m)], mz=low_bit(m)))
            return got

        raw_j = []
        for j in range(ob_j):
            block = jnp.stack([v[:, j] for v in cols])
            block = block.reshape(np_ * 2 * pieces, half)
            raw_j.append(gather_z(block))

        rows = jnp.stack(rows)
        cut = nz // 2
        got = {0: (rows[:cut], rows[cut:])}
        for m in range(1, np_):
            if m == low_bit(m):
                full = grid.swap(rows, mp=m)
                got[m] = (full[:cut], full[cut:])
            else:
                lo, hi = low_bit(m), high_bit(m)
                got[m] = (grid.swap(got[m ^ lo][0], mp=lo), grid.swap(got[m ^ hi][1], mp=hi))
        parts = [
            jnp.stack([got[m][h] for m in range(np_)], axis=1) for h in range(2)
        ]
        raw_i = jnp.concatenate(parts, axis=0)
        raw_i = raw_i.transpose(3, 0, 1, 2, 4, 5).reshape(ob_i, aux_total, half)

        def fit(block):
            return dot(block, metric, 0, 0).astype(BF16)

        fit_i = [fit(raw_i[i]) for i in range(ob_i)]
        fit_i_other = [grid.swap(f, mc=1) for f in fit_i]
        fit_j = [fit(jnp.concatenate(raw_j[j], axis=0)) for j in range(ob_j)]
        fit_j_other = [grid.swap(f, mc=1) for f in fit_j]

        eps_own = lax.dynamic_slice_in_dim(eps_vir, c * half, half, 0)
        eps_oth = lax.dynamic_slice_in_dim(eps_vir, (1 - c) * half, half, 0)
        eps_b = jnp.concatenate([eps_own, eps_oth])
        eps_i = lax.dynamic_slice_in_dim(eps_occ, z * ob_i, ob_i, 0)
        eps_j = lax.dynamic_slice_in_dim(eps_occ, plane * ob_j, ob_j, 0)

        q_rows = aux_total // (2 * nx)
        rows_own = jnp.stack(fit_i)
        rows_oth = jnp.stack(fit_i_other)
        amps = []
        for j in range(ob_j):
            amp = amplitude(
                rows_own, rows_oth, fit_j[j], fit_j_other[j], eps_own, eps_b, eps_i, eps_j[j]
            )
            amps.append((amp, grid.swap(amp, mc=1)))

        fits = list(zip(fit_j, fit_j_other))
        where = jnp.stack([x, c, c ^ y]).astype(jnp.int32)
        keep_x, keep_y = [], []
        for i in range(ob_i):
            kx, sx, ky, sy = gamma_terms(where, fits, amps, i, nx, q_rows)
            for m in range(1, nx):
                kx = kx + grid.swap(sx[m - 1], mp=m * ny).astype(F32)
            ky = ky + grid.swap(sy, mp=1).astype(F32)
            keep_x.append(kx)
            keep_y.append(ky)
        sum_x = jnp.stack(keep_x, axis=1)
        sum_y = jnp.stack(keep_y, axis=1)
        out_x = sum_x[0] + grid.swap(sum_x[1].astype(BF16), mp=1).astype(F32)
        out_y = sum_y[0]
        for m in range(1, nx):
            out_y = out_y + grid.swap(sum_y[m].astype(BF16), mp=m * ny).astype(F32)
        out = jnp.concatenate([out_x, out_y], axis=1)
        return out.transpose(2, 0, 1)

    return body


def solution(mesh):
    body = make_body(Grid(mesh))
    in_specs = (P(AXES, None, None), P(), P(), P())
    return jax.shard_map(
        body, mesh=mesh, in_specs=in_specs, out_specs=P("ja", "ia", "aux"), check_vma=False
    )
```
